32 devices in a mesh: grp: 2 (over x), exp: 16 (over z, y, core).
Axes of the slice: x: 2, y: 2, z: 4, core: 2. Of those that a mesh axis runs over, the one named last changes fastest.
Arguments:
- hidden: bfloat16 [32, 4096], P(('grp', 'exp')), may hold values from -6 to 6
- route_ids: int32 [32, 8], P(('grp', 'exp')), may hold values from 0 to 15, all different within a row; in each aligned block of 32 rows (0 to 31, 32 to 63, ...) at most 32 rows name the same one
- route_logits: bfloat16 [32, 8], P(('grp', 'exp')), may hold values from -6 to 6
- sampled: int32 [32], P(('grp', 'exp')), may hold values from 0 to 131071
- norm_gain: float32 [4096], replicated, may hold values from 0.5 to 1.5
- gate_weight: bfloat16 [16, 4096, 1536], P('exp', 'grp'), may hold values from -0.09375 to 0.09375
- up_weight: bfloat16 [16, 4096, 1536], P('exp', 'grp'), may hold values from -0.09375 to 0.09375
- down_weight: bfloat16 [16, 1536, 4096], P('exp', None, 'grp'), may hold values from -0.15625 to 0.15625
- head_weight: bfloat16 [4096, 131072], P(None, ('grp', 'exp')), may hold values from -0.25 to 0.25
- noise_steps: int32 [131072], P(('grp', 'exp')), may hold values from -64 to 64
Outputs:
- vote_counts: float32 [131072], P(('grp', 'exp'))
- log_ratio: float32 [32], P(('grp', 'exp'))
The draws below stay inside these ranges and needn't reach their ends.
Inputs may be any that keep to these rules, and one draw needn't show every extreme that they name: `route_ids`: each row names 8 different experts. Over all 32 rows no expert is named by more than 32 rows, a bound that some block reaches.
All inputs are finite; a program needn't handle non-finite values.
Results may differ from the reference program's by a relative error of at most 0.004.
Values may be sent and summed in bfloat16 or wider, within the bound.
A program may use at most 128 MiB of HBM per device.

```python
import math
import jax
import jax.numpy as jnp
import numpy as np
from jax import lax

D = 4096
FF = 1536
TOPK = 8
VOCAB = 131072
MEMBERS = 32
EXPERTS = 16
CAP = 32


def set_ends(drawn, stream_key, smallest, largest):
    longest = drawn.shape.index(max(drawn.shape))
    spots = []
    for shift in (0, 1):
        where = [jax.random.randint(jax.random.fold_in(stream_key, axis), (), 0, length) for axis, length in enumerate(drawn.shape)]
        where[longest] = (where[longest] + shift) % drawn.shape[longest]
        spots.append(tuple(where))
    return drawn.at[spots[0]].set(smallest).at[spots[1]].set(largest)


def block_scale(own_key, dims, pieces, least, high):
    gain = 1.0
    for dim, blocks in pieces:
        steps = jax.random.uniform(jax.random.fold_in(jax.random.fold_in(own_key, 6), dim), (blocks,), jnp.float32, least / len(pieces), high / len(pieces))
        gain = gain * jnp.repeat(jnp.exp(steps), dims[dim] // blocks).reshape((-1,) + (1,) * (len(dims) - 1 - dim))
    return gain


def deal_out(rng, own, number, rows, count, top, reach, slope):
    ranking = jax.random.permutation(rng, count)
    crowded, common = load_shares(count, rows * top, reach, slope, True), load_shares(count, rows * top, reach, slope, False)
    places = jnp.arange(count)

    def named(sizes, offset_by):
        used = int((sizes > 0).sum())
        fixed = max(1, used // 4)
        moved = fixed + (places - fixed + offset_by * (used - fixed)) % max(1, count - fixed)
        return jnp.zeros((count,), jnp.int32).at[ranking[jnp.where(places < fixed, places, moved)]].set(jnp.asarray(sizes, jnp.int32))

    sizes = jnp.where(number % 4 == 0, named(crowded, number // 4), named(common, number - number // 4 - 1))
    mixed = jax.random.permutation(jax.random.fold_in(own, 3), count)
    giver, sink = mixed[0:count // 2 * 2:2], mixed[1:count // 2 * 2:2]
    margin = jnp.minimum(sizes[giver] - 1, reach - sizes[sink]) // 2
    margin = jnp.where((giver == ranking[0]) | (sink == ranking[0]) | (sizes[sink] == 0), 0, jnp.maximum(margin, 0))
    moved = jax.random.randint(jax.random.fold_in(own, 4), (count // 2,), 0, 1 << 20) % (margin + 1)
    sizes = sizes.at[giver].add(-moved).at[sink].add(moved)
    items = jnp.searchsorted(jnp.cumsum(sizes), jnp.arange(rows * top), side="right").astype(jnp.int32)
    grid = items.reshape(top, rows).T
    grid = grid[jax.random.permutation(jax.random.fold_in(own, 1), rows)]
    offset_by = jax.random.randint(jax.random.fold_in(own, 2), (rows, 1), 0, top)
    return jnp.take_along_axis(grid, (jnp.arange(top)[None, :] + offset_by) % top, axis=1)


def load_shares(amount, total, most, lean, full):
    portions = [(1 << 20) // math.isqrt(standing ** lean) + 1 for standing in range(1, amount + 1)]
    largest = most if full else min(most, max(-(-total // amount), total * portions[0] // sum(portions)))
    least = 1 if total - largest >= amount - 1 else 0
    given, surplus = [largest] + [least] * (amount - 1), total - largest - least * (amount - 1)
    while surplus > 0:
        movable = [i for i in range(1, amount) if given[i] < largest] or [i for i in range(1, amount) if given[i] < most]
        pool, remaining = sum([portions[i] for i in movable]), surplus
        for i in movable:
            more = min(most - given[i], max(1, remaining * portions[i] // pool), surplus)
            given[i] = given[i] + more
            surplus = surplus - more
    return np.array(given)


def centred(rng, shape, deviation, bound, shards=(), kind=jnp.bfloat16):
    level = block_scale(rng, shape, shards, -0.22, 0.18) if shards else 1.0
    result = jax.random.normal(rng, shape, jnp.float32) * deviation * level
    return jnp.minimum(jnp.maximum(result, -bound), bound).astype(kind)


def setup_inputs(seed: int = 0) -> dict:
    key_of = jax.random.split(jax.random.key(seed), 11)
    hidden = centred(key_of[0], (MEMBERS, D), 1.0, 6.0, ((0, 32),))
    route_ids_keys = jax.random.split(jax.random.fold_in(key_of[1], 1), MEMBERS // MEMBERS)
    route_ids_turns = jax.random.permutation(jax.random.fold_in(key_of[1], 3), MEMBERS // MEMBERS)
    route_ids = jax.vmap(lambda own, number: deal_out(jax.random.fold_in(key_of[1], 2), own, number, MEMBERS, EXPERTS, TOPK, CAP, 2))(route_ids_keys, route_ids_turns).reshape((MEMBERS, TOPK))
    route_logits = centred(key_of[2], (MEMBERS, TOPK), 1.0, 6.0, ((0, 32),))
    sampled = set_ends(jax.random.randint(key_of[3], (MEMBERS,), 0, VOCAB), jax.random.fold_in(key_of[3], 1), 0, VOCAB - 1).astype(jnp.int32)
    norm_gain = jnp.clip(1.0 + 0.1 * jax.random.normal(key_of[4], (D,), jnp.float32), 0.5, 1.5)
    gate_weight = centred(key_of[5], (EXPERTS, D, FF), D ** -0.5, 0.09375, ((0, 16), (1, 2)))
    up_weight = centred(key_of[6], (EXPERTS, D, FF), D ** -0.5, 0.09375, ((0, 16), (1, 2)))
    down_weight = centred(key_of[7], (EXPERTS, FF, D), FF ** -0.5, 0.15625, ((0, 16), (2, 2)))
    head_weight = centred(key_of[8], (D, VOCAB), (D // 9) ** -0.5, 0.25, ((1, 32),))
    noise_steps = set_ends(jax.random.randint(key_of[9], (VOCAB,), -64, 65), jax.random.fold_in(key_of[9], 1), -64, 64).astype(jnp.int32)
    return dict(hidden=hidden, route_ids=route_ids, route_logits=route_logits, sampled=sampled, norm_gain=norm_gain, gate_weight=gate_weight, up_weight=up_weight, down_weight=down_weight, head_weight=head_weight, noise_steps=noise_steps)


clip_bound = 8.0
noise_step = 0.03125
norm_eps = 1e-06

def slot_matrix(route_ids, expert):
    chosen = jnp.any(route_ids == expert, axis=1)
    position = jnp.cumsum(chosen.astype(jnp.int32)).astype(jnp.int32) - 1
    slot_index = jnp.arange(CAP, dtype=jnp.int32)
    select = (position[None, :] == slot_index[:, None]) & chosen[None, :]
    return select.astype(jnp.bfloat16)

def reference(hidden, route_ids, route_logits, sampled, norm_gain, gate_weight, up_weight, down_weight, head_weight, noise_steps):
    mixing = jax.nn.softmax(route_logits.astype(jnp.float32), axis=-1)

    def expert_step(moe_total, expert):
        select = slot_matrix(route_ids, expert)
        share = lax.optimization_barrier(jnp.sum(jnp.where(route_ids == expert, mixing, 0.0), axis=1))
        picked = jnp.dot(select, hidden, preferred_element_type=jnp.float32).astype(jnp.bfloat16)
        gate = jnp.dot(picked, gate_weight[expert], preferred_element_type=jnp.float32)
        upward = jnp.dot(picked, up_weight[expert], preferred_element_type=jnp.float32)
        active = (jax.nn.silu(gate) * upward).astype(jnp.bfloat16)
        output = jnp.dot(active, down_weight[expert], preferred_element_type=jnp.float32).astype(jnp.bfloat16)
        spread = jnp.dot(select.T, output, preferred_element_type=jnp.float32)
        return (moe_total + spread * share[:, None], None)
    moe_total, unused = lax.scan(expert_step, jnp.zeros(hidden.shape, jnp.float32), jnp.arange(EXPERTS, dtype=jnp.int32))
    residual = (hidden.astype(jnp.float32) + moe_total).astype(jnp.bfloat16)
    scaled = (residual.astype(jnp.float32) * norm_gain[None, :]).astype(jnp.bfloat16)
    squares = lax.optimization_barrier(jnp.sum(jnp.square(residual.astype(jnp.float32)), axis=1))
    root_mean = jnp.sqrt(squares / D + norm_eps)
    logits = jnp.dot(scaled, head_weight, preferred_element_type=jnp.float32) / root_mean[:, None]
    clipped = jnp.clip(logits, -clip_bound, clip_bound)
    exp_values = jnp.exp(clipped)
    totals = lax.optimization_barrier(jnp.sum(exp_values, axis=1))
    chosen_logit = jnp.take_along_axis(clipped, sampled[:, None].astype(jnp.int32), axis=1)[:, 0]
    log_ratio = chosen_logit - jnp.log(totals / VOCAB)
    vote_counts = VOCAB / MEMBERS * lax.optimization_barrier(jnp.sum(exp_values / totals[:, None], axis=0)) + noise_steps.astype(jnp.float32) * noise_step
    return (vote_counts, log_ratio)
```

```python
import functools

import jax
import jax.numpy as jnp
from jax import lax
from jax.experimental import pallas as pl
from jax.experimental.pallas import tpu as pltpu
from jax.sharding import PartitionSpec as P

TOPK = 8
VOCAB = 131072


clip_bound = 8.0
noise_step = 0.03125
norm_eps = 1e-06


def on_device_general(
    hidden,
    route_ids,
    route_logits,
    sampled,
    norm_gain,
    gate_weight,
    up_weight,
    down_weight,
    head_weight,
    noise_steps,
):
    groups = lax.axis_size("grp")
    columns_count = lax.axis_size("exp")
    width = gate_weight.shape[1]
    column_index = lax.axis_index("exp")
    device_index = lax.axis_index(("grp", "exp"))
    group_rows, group_ids, group_logits, group_sampled = (
        lax.all_gather(hidden, "exp", axis=0, tiled=True),
        lax.all_gather(route_ids, "exp", axis=0, tiled=True),
        lax.all_gather(route_logits, "exp", axis=0, tiled=True),
        lax.all_gather(sampled, "exp", axis=0, tiled=True),
    )
    row_count = group_rows.shape[0]
    topk_width = group_ids.shape[1]
    pieces = group_rows.reshape(row_count, groups, width)
    ids_spread = jnp.broadcast_to(group_ids[:, None, :], (row_count, groups, topk_width))
    logits_spread = jnp.broadcast_to(group_logits[:, None, :], (row_count, groups, topk_width))
    sampled_spread = jnp.broadcast_to(group_sampled[:, None, None], (row_count, groups, 1))
    arrived = (
        lax.all_to_all(pieces, "grp", split_axis=1, concat_axis=0, tiled=True),
        lax.all_to_all(ids_spread, "grp", split_axis=1, concat_axis=0, tiled=True),
        lax.all_to_all(logits_spread, "grp", split_axis=1, concat_axis=0, tiled=True),
        lax.all_to_all(sampled_spread, "grp", split_axis=1, concat_axis=0, tiled=True),
    )
    member_count = row_count * groups
    width_slab = arrived[0].reshape(member_count, width)
    ids_all = arrived[1].reshape(member_count, topk_width)
    logits_all = arrived[2].reshape(member_count, topk_width)
    sampled_all = arrived[3].reshape(member_count)
    members_total = width_slab.shape[0]
    capacity = min(members_total, 2 * members_total * TOPK // columns_count)
    mixing = jax.nn.softmax(logits_all.astype(jnp.float32), axis=-1)
    matches = ids_all == column_index
    chosen = jnp.any(matches, axis=1)
    share = jnp.sum(jnp.where(matches, mixing, 0.0), axis=1)
    position = jnp.cumsum(chosen.astype(jnp.int32)) - 1
    slot_index = jnp.arange(capacity, dtype=jnp.int32)
    select = ((position[None, :] == slot_index[:, None]) & chosen[None, :]).astype(jnp.bfloat16)
    picked = jnp.dot(select, width_slab, preferred_element_type=jnp.float32).astype(jnp.bfloat16)
    gate_part = jnp.dot(picked, gate_weight[0], preferred_element_type=jnp.float32)
    upward_part = jnp.dot(picked, up_weight[0], preferred_element_type=jnp.float32)
    gate_sum, upward_sum = lax.psum((gate_part, upward_part), "grp")
    active = (jax.nn.silu(gate_sum) * upward_sum).astype(jnp.bfloat16)
    output = jnp.dot(active, down_weight[0], preferred_element_type=jnp.float32).astype(
        jnp.bfloat16
    )
    spread = jnp.einsum("cm,cw->mw", select, output, preferred_element_type=jnp.float32)
    contrib = spread * share[:, None]
    moe_slab = lax.psum(contrib, "exp")
    residual = (width_slab.astype(jnp.float32) + moe_slab).astype(jnp.bfloat16)
    vocab_block = head_weight.shape[1]
    piece = lax.all_gather(residual, "grp", axis=1, tiled=True)
    scaled = (piece.astype(jnp.float32) * norm_gain[None, :]).astype(jnp.bfloat16)
    acc_logits = jnp.dot(scaled, head_weight, preferred_element_type=jnp.float32)
    acc_squares = jnp.sum(jnp.square(piece.astype(jnp.float32)), axis=1)
    model_width = norm_gain.shape[0]
    root_mean = jnp.sqrt(acc_squares / model_width + norm_eps)
    logits = acc_logits / root_mean[:, None]
    clipped = jnp.clip(logits, -clip_bound, clip_bound)
    exp_values = jnp.exp(clipped)
    first_column = device_index * vocab_block
    vocab_columns = first_column + jnp.arange(vocab_block, dtype=jnp.int32)
    owned = sampled_all[:, None] == vocab_columns[None, :]
    part_total = jnp.sum(exp_values, axis=1)
    part_chosen = jnp.sum(jnp.where(owned, clipped, 0.0), axis=1)
    totals, chosen_logit = lax.psum((part_total, part_chosen), ("grp", "exp"))
    log_ratio = chosen_logit - jnp.log(totals / VOCAB)
    own_rows = hidden.shape[0]
    own_ratio = lax.dynamic_slice_in_dim(log_ratio, device_index * own_rows, own_rows, 0)
    vote_counts = (
        VOCAB / members_total * jnp.sum(exp_values / totals[:, None], axis=0)
        + noise_steps.astype(jnp.float32) * noise_step
    )
    return (vote_counts, own_ratio)


MESH = pl.DeviceIdType.MESH
LANES = 128
FF_CHUNK = 512
OUT_CHUNK = 512
HEAD_ROWS = 512
HEAD_CHUNK = 512
VMEM_BYTES = 62 * 1024 * 1024


def plane_order(plane, planes):
    if planes != 4:
        return [lax.rem(plane + t, planes) for t in range(planes)]
    half = lax.div(plane, 2)
    return [plane, plane + 1 - 2 * lax.rem(plane, 2), 2 - half, 3 - 3 * half]


def fused_kernel(
    groups,
    experts,
    hidden_ref,
    ids_ref,
    logits_ref,
    sampled_ref,
    gain_ref,
    gate_hbm,
    up_hbm,
    down_hbm,
    head_hbm,
    votes_ref,
    ratio_ref,
    gate_w,
    up_w,
    down_w,
    head_w,
    row_f32,
    row_stage,
    rows_in,
    rows_f32,
    slab,
    meta_out,
    meta_in,
    part_own,
    part_out,
    part_in,
    active,
    contrib,
    contrib_in,
    block_out,
    residual,
    scaled,
    exps,
    sums_out,
    sums_in,
    gu_sem,
    down_sem,
    head_sem,
    rows_send,
    rows_recv,
    meta_send,
    meta_recv,
    part_send,
    part_recv,
    contrib_send,
    contrib_recv,
    block_send,
    block_recv,
    relay_send,
    sums_send,
    sums_recv,
):
    g = lax.axis_index("grp")
    e = lax.axis_index("exp")
    count = groups * experts
    me = g * experts + e
    width = slab.shape[1]
    ff = part_own.shape[2]
    model = residual.shape[1]
    vocab_block = head_w.shape[1]
    pieces = width // LANES

    gu_copies = []
    for c in range(ff // FF_CHUNK):
        cols = pl.ds(c * FF_CHUNK, FF_CHUNK)
        a = pltpu.make_async_copy(gate_hbm.at[0, :, cols], gate_w.at[:, cols], gu_sem.at[2 * c])
        b = pltpu.make_async_copy(up_hbm.at[0, :, cols], up_w.at[:, cols], gu_sem.at[2 * c + 1])
        a.start()
        b.start()
        gu_copies.append((a, b))
    down_copy = pltpu.make_async_copy(down_hbm.at[0], down_w, down_sem.at[0])
    down_copy.start()
    head_copies = []
    for c in range(model // HEAD_ROWS):
        rows = pl.ds(c * HEAD_ROWS, HEAD_ROWS)
        a = pltpu.make_async_copy(head_hbm.at[rows, :], head_w.at[rows, :], head_sem.at[c])
        a.start()
        head_copies.append(a)

    def peer_of(k):
        peer = lax.rem(me + k, count)
        return peer, lax.div(peer, experts), lax.rem(peer, experts)

    barrier = pltpu.get_barrier_semaphore()

    def greet(k, carry):
        peer, pg, pe = peer_of(k)
        pl.semaphore_signal(barrier, inc=1, device_id=(pg, pe), device_id_type=MESH)
        return carry

    lax.fori_loop(1, count, greet, 0)

    row = hidden_ref[...].astype(jnp.float32)
    for c in range(model // LANES):
        row_f32[c : c + 1, :] = row[:, c * LANES : (c + 1) * LANES]
    for h in range(groups):
        row_stage[h] = row_f32[h * pieces : (h + 1) * pieces, :].astype(jnp.bfloat16)
    lane = lax.broadcasted_iota(jnp.int32, (1, LANES), 1)
    scores = logits_ref[...].astype(jnp.float32)
    shifted = jnp.exp(scores - jnp.max(scores, axis=1, keepdims=True))
    mixing = shifted / jnp.sum(shifted, axis=1, keepdims=True)
    ids = ids_ref[...]
    meta = jnp.where(lane == experts, sampled_ref[...].astype(jnp.float32), 0.0)
    for k in range(ids.shape[1]):
        meta = meta + jnp.where(lane == ids[:, k : k + 1], mixing[:, k : k + 1], 0.0)
    meta_out[...] = meta
    meta_in[me] = meta
    rows_in[me] = row_stage[g]

    pl.semaphore_wait(barrier, count - 1)

    def rows_copy(k, sender):
        peer, pg, pe = peer_of(k)
        slot = me if sender else peer
        return pltpu.make_async_remote_copy(
            src_ref=row_stage.at[pg],
            dst_ref=rows_in.at[slot],
            send_sem=rows_send.at[k],
            recv_sem=rows_recv.at[slot],
            device_id=(pg, pe),
            device_id_type=MESH,
        )

    def meta_copy(k, sender):
        peer, pg, pe = peer_of(k)
        slot = me if sender else peer
        return pltpu.make_async_remote_copy(
            src_ref=meta_out,
            dst_ref=meta_in.at[slot],
            send_sem=meta_send.at[k],
            recv_sem=meta_recv.at[slot],
            device_id=(pg, pe),
            device_id_type=MESH,
        )

    def each(low, high, action):
        def step(k, carry):
            action(k)
            return carry

        lax.fori_loop(low, high, step, 0)

    each(1, count, lambda k: rows_copy(k, True).start())
    each(1, count, lambda k: meta_copy(k, True).start())
    each(1, count, lambda k: rows_copy(k, False).wait_recv())

    for m in range(count):
        rows_f32[m * pieces : (m + 1) * pieces, :] = rows_in[m].astype(jnp.float32)
    for c in range(pieces):
        slab[:, c * LANES : (c + 1) * LANES] = rows_f32[
            pl.ds(c, count, stride=pieces), :
        ].astype(jnp.bfloat16)

    def part_copy(c, k, sender):
        og = lax.rem(g + k, groups)
        slot = g if sender else og
        return pltpu.make_async_remote_copy(
            src_ref=part_out.at[c],
            dst_ref=part_in.at[slot, c],
            send_sem=part_send.at[k, c],
            recv_sem=part_recv.at[slot, c],
            device_id=(og, e),
            device_id_type=MESH,
        )

    for c in range(ff // FF_CHUNK):
        cols = slice(c * FF_CHUNK, (c + 1) * FF_CHUNK)
        for i, (copy, weight) in enumerate(zip(gu_copies[c], (gate_w, up_w))):
            copy.wait()
            value = jnp.dot(slab[...], weight[:, cols], preferred_element_type=jnp.float32)
            part_own[i, :, cols] = value
            part_out[c, i] = value.astype(jnp.bfloat16)
        for k in range(1, groups):
            part_copy(c, k, True).start()

    each(1, count, lambda k: meta_copy(k, False).wait_recv())
    metas = jnp.concatenate([meta_in[m] for m in range(count)], axis=0)
    wide_lane = lax.broadcasted_iota(jnp.int32, (count, LANES), 1)
    share = jnp.sum(jnp.where(wide_lane == e, metas, 0.0), axis=1, keepdims=True)
    wanted = jnp.sum(jnp.where(wide_lane == experts, metas, 0.0), axis=1, keepdims=True)

    for c in range(ff // FF_CHUNK):
        cols = slice(c * FF_CHUNK, (c + 1) * FF_CHUNK)
        gate, upward = part_own[0, :, cols], part_own[1, :, cols]
        for k in range(1, groups):
            part_copy(c, k, False).wait_recv()
            og = lax.rem(g + k, groups)
            gate = gate + part_in[og, c, 0].astype(jnp.float32)
            upward = upward + part_in[og, c, 1].astype(jnp.float32)
        active[:, cols] = (gate / (1.0 + jnp.exp(-gate)) * upward).astype(jnp.bfloat16)

    quad = OUT_CHUNK // LANES
    plane, corner = lax.div(e, quad), lax.rem(e, quad)
    parity = lax.rem(corner, 2)
    row_in_plane = lax.div(corner, 2)
    order = plane_order(plane, experts // quad)

    def contrib_copy(t, p, sender):
        there = lax.rem(corner + p, quad)
        oe = order[t] * quad + there
        slot = e if sender else oe
        return pltpu.make_async_remote_copy(
            src_ref=contrib.at[t * quad + there],
            dst_ref=contrib_in.at[slot],
            send_sem=contrib_send.at[t * quad + p],
            recv_sem=contrib_recv.at[slot],
            device_id=(g, oe),
            device_id_type=MESH,
        )

    steps = len(order)
    down_copy.wait()
    for t in reversed(range(steps)):
        cols = pl.ds(pl.multiple_of(order[t] * OUT_CHUNK, OUT_CHUNK), OUT_CHUNK)
        value = jnp.dot(active[...], down_w[:, cols], preferred_element_type=jnp.float32)
        value = value.astype(jnp.bfloat16).astype(jnp.float32) * share
        value = value.astype(jnp.bfloat16)
        for p in range(quad):
            contrib[t * quad + p] = value[:, p * LANES : (p + 1) * LANES]
        for p in range(0 if t else 1, quad):
            contrib_copy(t, p, True).start()
    mine = pl.ds(pl.multiple_of(e * LANES, LANES), LANES)
    total = slab[:, mine].astype(jnp.float32)
    moe = contrib[corner].astype(jnp.float32)
    for t in range(steps):
        for p in range(0 if t else 1, quad):
            contrib_copy(t, p, False).wait_recv()
            there = order[t] * quad + lax.rem(corner + p, quad)
            moe = moe + contrib_in[there].astype(jnp.float32)
    block = (total + moe).astype(jnp.bfloat16)
    block_out[...] = block

    def columns_of(slot):
        return pl.ds(pl.multiple_of(slot * LANES, LANES), LANES)

    def block_copy(t, a, b, sender):
        og = lax.rem(g + a, groups)
        oe = order[t] * quad + 2 * lax.rem(row_in_plane + b, quad // 2) + parity
        slot = me if sender else og * experts + oe
        n = (t * groups + a) * (quad // 2) + b
        return pltpu.make_async_remote_copy(
            src_ref=block_out,
            dst_ref=residual.at[:, columns_of(slot)],
            send_sem=block_send.at[n],
            recv_sem=block_recv.at[slot],
            device_id=(og, oe),
            device_id_type=MESH,
        )

    def relay_copy(t, a, b, sender):
        og = lax.rem(g + a, groups)
        pair = order[t] * quad + 2 * lax.rem(row_in_plane + b, quad // 2)
        slot = og * experts + pair + (parity if sender else 1 - parity)
        n = (t * groups + a) * (quad // 2) + b
        own = sender and (t, a, b) == (0, 0, 0)
        return pltpu.make_async_remote_copy(
            src_ref=block_out if own else residual.at[:, columns_of(slot)],
            dst_ref=residual.at[:, columns_of(slot)],
            send_sem=relay_send.at[n],
            recv_sem=block_recv.at[slot],
            device_id=(g, e + 1 - 2 * parity),
            device_id_type=MESH,
        )

    spots = [(a, b) for a in range(groups) for b in range(quad // 2)]
    for t in reversed(range(steps)):
        for a, b in spots:
            if (t, a, b) != (0, 0, 0):
                block_copy(t, a, b, True).start()
    relay_copy(0, 0, 0, True).start()
    residual[:, columns_of(me)] = block

    def relay(t):
        for a, b in spots:
            if (t, a, b) != (0, 0, 0):
                block_copy(t, a, b, False).wait_recv()
                relay_copy(t, a, b, True).start()

    first = wanted - (me * vocab_block).astype(jnp.float32)
    depth = groups * OUT_CHUNK
    squares = jnp.zeros((count, LANES), jnp.float32)
    zero = jnp.zeros((count, LANES), jnp.float32)
    for copy in head_copies:
        copy.wait()
    relay(0)
    for t in range(steps):
        if t + 1 < steps:
            relay(t + 1)
        for a, b in spots:
            relay_copy(t, a, b, False).wait_recv()
        starts = [pl.multiple_of(h * width + order[t] * OUT_CHUNK, OUT_CHUNK) for h in range(groups)]
        for h in range(groups):
            for p in range(quad):
                cols = pl.ds(pl.multiple_of(starts[h] + p * LANES, LANES), LANES)
                value = residual[:, cols].astype(jnp.float32)
                squares = squares + value * value
                at = t * depth + h * OUT_CHUNK + p * LANES
                scaled[:, at : at + LANES] = (value * gain_ref[:, cols]).astype(jnp.bfloat16)

        def product(cols, t=t, starts=starts):
            value = None
            for h in range(groups):
                at = t * depth + h * OUT_CHUNK
                part = jnp.dot(
                    scaled[:, at : at + OUT_CHUNK],
                    head_w[pl.ds(starts[h], OUT_CHUNK), cols],
                    preferred_element_type=jnp.float32,
                )
                value = part if value is None else value + part
            return value if t == 0 else value + exps[:, cols]

        if t + 1 < steps:

            def gather_step(c, carry, product=product):
                cols = pl.ds(pl.multiple_of(c * HEAD_CHUNK, HEAD_CHUNK), HEAD_CHUNK)
                exps[:, cols] = product(cols)
                return carry

            lax.fori_loop(0, vocab_block // HEAD_CHUNK, gather_step, 0)
            continue

        mean = jnp.sum(squares, axis=1, keepdims=True) / model
        inverse = 1.0 / jnp.sqrt(mean + norm_eps)

        def head_step(c, carry, product=product, inverse=inverse):
            sums, picked = carry
            cols = pl.ds(pl.multiple_of(c * HEAD_CHUNK, HEAD_CHUNK), HEAD_CHUNK)
            value = jnp.clip(product(cols) * inverse, -clip_bound, clip_bound)
            grown = jnp.exp(value)
            exps[:, cols] = grown
            column = lax.broadcasted_iota(jnp.int32, (count, HEAD_CHUNK), 1) + c * HEAD_CHUNK
            owned = jnp.where(column.astype(jnp.float32) == first, value, 0.0)
            for p in range(HEAD_CHUNK // LANES):
                part = slice(p * LANES, (p + 1) * LANES)
                sums = sums + grown[:, part]
                picked = picked + owned[:, part]
            return sums, picked

        sums, picked = lax.fori_loop(0, vocab_block // HEAD_CHUNK, head_step, (zero, zero))
    diagonal = lax.broadcasted_iota(jnp.int32, (count, LANES), 0) == wide_lane
    for i, value in enumerate((sums, picked)):
        column = jnp.sum(value, axis=1, keepdims=True)
        sums_out[i : i + 1, :] = jnp.sum(jnp.where(diagonal, column, 0.0), axis=0, keepdims=True)

    def sums_copy(k, sender):
        peer, pg, pe = peer_of(k)
        slot = me if sender else peer
        return pltpu.make_async_remote_copy(
            src_ref=sums_out,
            dst_ref=sums_in.at[slot],
            send_sem=sums_send.at[k],
            recv_sem=sums_recv.at[slot],
            device_id=(pg, pe),
            device_id_type=MESH,
        )

    each(1, count, lambda k: sums_copy(k, True).start())
    sums_in[me] = sums_out[...]
    each(1, count, lambda k: rows_copy(k, True).wait_send())
    each(1, count, lambda k: meta_copy(k, True).wait_send())
    for c in range(ff // FF_CHUNK):
        for k in range(1, groups):
            part_copy(c, k, True).wait_send()
    for t in range(steps):
        for p in range(0 if t else 1, quad):
            contrib_copy(t, p, True).wait_send()
        for a, b in spots:
            if (t, a, b) != (0, 0, 0):
                block_copy(t, a, b, True).wait_send()
            relay_copy(t, a, b, True).wait_send()
    each(1, count, lambda k: sums_copy(k, False).wait_recv())
    both = sums_in[0]
    for k in range(1, count):
        both = both + sums_in[k]
    totals, chosen = both[0:1], both[1:2]
    ratio = chosen - jnp.log(jnp.where(lane < count, totals, 1.0) / (vocab_block * count))
    ratio = jnp.sum(jnp.where(lane == me, ratio, 0.0), axis=1, keepdims=True)
    ratio_ref[...] = jnp.broadcast_to(ratio, ratio_ref.shape)
    weight = jnp.sum(jnp.where(diagonal, totals, 0.0), axis=1, keepdims=True)
    weight = vocab_block / weight
    for c in range(vocab_block // HEAD_CHUNK):
        cols = slice(c * HEAD_CHUNK, (c + 1) * HEAD_CHUNK)
        votes_ref[:, cols] = jnp.sum(exps[:, cols] * weight, axis=0, keepdims=True)
    each(1, count, lambda k: sums_copy(k, True).wait_send())


def fused(
    groups,
    experts,
    hidden,
    route_ids,
    route_logits,
    sampled,
    norm_gain,
    gate_weight,
    up_weight,
    down_weight,
    head_weight,
    noise_steps,
):
    count = groups * experts
    width, ff = gate_weight.shape[1:]
    model, vocab_block = head_weight.shape
    pieces = width // LANES
    chunks = ff // FF_CHUNK
    bf16, f32 = jnp.bfloat16, jnp.float32
    vmem = pl.BlockSpec(memory_space=pltpu.VMEM)
    hbm = pl.BlockSpec(memory_space=pl.ANY)
    dma = pltpu.SemaphoreType.DMA
    votes, ratio = pl.pallas_call(
        functools.partial(fused_kernel, groups, experts),
        out_shape=(
            jax.ShapeDtypeStruct((1, vocab_block), f32),
            jax.ShapeDtypeStruct((1, LANES), f32),
        ),
        in_specs=[vmem] * 5 + [hbm] * 4,
        out_specs=(vmem, vmem),
        scratch_shapes=[
            pltpu.VMEM((width, ff), bf16),
            pltpu.VMEM((width, ff), bf16),
            pltpu.VMEM((ff, width), bf16),
            pltpu.VMEM((model, vocab_block), bf16),
            pltpu.VMEM((model // LANES, LANES), f32),
            pltpu.VMEM((groups, pieces, LANES), bf16),
            pltpu.VMEM((count, pieces, LANES), bf16),
            pltpu.VMEM((count * pieces, LANES), f32),
            pltpu.VMEM((count, width), bf16),
            pltpu.VMEM((1, LANES), f32),
            pltpu.VMEM((count, 1, LANES), f32),
            pltpu.VMEM((2, count, ff), f32),
            pltpu.VMEM((chunks, 2, count, FF_CHUNK), bf16),
            pltpu.VMEM((groups, chunks, 2, count, FF_CHUNK), bf16),
            pltpu.VMEM((count, ff), bf16),
            pltpu.VMEM((experts, count, LANES), bf16),
            pltpu.VMEM((experts, count, LANES), bf16),
            pltpu.VMEM((count, LANES), bf16),
            pltpu.VMEM((count, model), bf16),
            pltpu.VMEM((count, model), bf16),
            pltpu.VMEM((count, vocab_block), f32),
            pltpu.VMEM((2, LANES), f32),
            pltpu.VMEM((count, 2, LANES), f32),
            dma((2 * chunks,)),
            dma((1,)),
            dma((model // HEAD_ROWS,)),
            dma((count,)),
            dma((count,)),
            dma((count,)),
            dma((count,)),
            dma((groups, chunks)),
            dma((groups, chunks)),
            dma((experts,)),
            dma((experts,)),
            dma((count,)),
            dma((count,)),
            dma((count,)),
            dma((count,)),
            dma((count,)),
        ],
        compiler_params=pltpu.CompilerParams(
            collective_id=0, has_side_effects=True, vmem_limit_bytes=VMEM_BYTES
        ),
    )(
        hidden,
        route_ids,
        route_logits,
        sampled.reshape(1, 1),
        norm_gain.reshape(1, model),
        gate_weight,
        up_weight,
        down_weight,
        head_weight,
    )
    vote_counts = votes.reshape(vocab_block) + noise_steps.astype(f32) * noise_step
    return (vote_counts, ratio[0, :1])


def on_device(hidden, route_ids, route_logits, sampled, norm_gain, *weights):
    groups, experts = lax.axis_size("grp"), lax.axis_size("exp")
    count = groups * experts
    width, ff = weights[0].shape[1:]
    model, vocab_block = weights[3].shape
    held = 2 * (3 * width * ff + model * vocab_block)
    fits = (
        hidden.shape[0] == 1
        and weights[0].shape[0] == 1
        and width == experts * LANES
        and model == groups * width
        and width % (16 * LANES) == 0
        and ff % FF_CHUNK == 0
        and width % OUT_CHUNK == 0
        and model % HEAD_ROWS == 0
        and vocab_block % HEAD_CHUNK == 0
        and count % 16 == 0
        and experts % (OUT_CHUNK // LANES) == 0
        and OUT_CHUNK // LANES % 2 == 0
        and count <= LANES
        and held <= 54 * 1024 * 1024
    )
    whole = (hidden, route_ids, route_logits, sampled, norm_gain, *weights)
    if fits:
        return fused(groups, experts, *whole)
    return on_device_general(*whole)


def solution(mesh):
    placed = (
        P(("grp", "exp"), None),
        P(("grp", "exp"), None),
        P(("grp", "exp"), None),
        P(("grp", "exp")),
        P(),
        P("exp", "grp", None),
        P("exp", "grp", None),
        P("exp", None, "grp"),
        P(None, ("grp", "exp")),
        P(("grp", "exp")),
    )
    return jax.shard_map(
        on_device,
        mesh=mesh,
        in_specs=placed,
        out_specs=(P(("grp", "exp")), P(("grp", "exp"))),
        check_vma=False,
    )
```
